32 devices in a mesh: groups: 2 (over y), latent: 4 (over z), rows: 4 (over x, core).
Axes of the slice: x: 2, y: 2, z: 4, core: 2. Of those that a mesh axis runs over, the one named last changes fastest.
Arguments:
- activations_in: bfloat16 [2, 128, 2304], P('groups', None, 'latent'), parts along dimension 0, may hold values from -6 to 6
- gate_proj: bfloat16 [2304, 4608], P('rows', 'latent'), may hold values from -0.125 to 0.125
- up_proj: bfloat16 [2304, 4608], P('rows', 'latent'), may hold values from -0.125 to 0.125
- down_proj: bfloat16 [4608, 2304], P('latent', 'rows'), may hold values from -0.09375 to 0.09375
- enc_weight: bfloat16 [4608, 65536], P(('groups', 'rows'), 'latent'), parts along dimension 0, may hold values from -6 to 6
- enc_bias: float32 [131072], P(('groups', 'latent')), parts along dimension 0, may hold values from -0.5 to 0.5
- dec_weight: bfloat16 [131072, 2304], P(('groups', 'latent'), 'rows'), parts along dimension 0, may hold values from -6 to 6
- dec_bias: float32 [4608], P(('groups', 'rows')), parts along dimension 0, may hold values from -0.5 to 0.5
Outputs:
- enc_weight_new: bfloat16 [4608, 65536], P(('groups', 'rows'), 'latent'), parts along dimension 0
- enc_bias_new: float32 [131072], P(('groups', 'latent')), parts along dimension 0
- dec_weight_new: bfloat16 [131072, 2304], P(('groups', 'latent'), 'rows'), parts along dimension 0
- dec_bias_new: float32 [4608], P(('groups', 'rows')), parts along dimension 0
The draws below stay inside these ranges and needn't reach their ends.
There are 2 independent parts, one for each index of `groups`. The reference program is written for one: setup_inputs(seed, part) draws one part's arguments, and reference() takes and returns one part's arrays. A program takes and returns all parts, laid end to end along the dimension named above; an argument that names none is the same for every part. Nothing has to cross between parts.
All inputs are finite; a program needn't handle non-finite values.
Results may differ from the reference program's by a relative error of at most 0.02.
Values may be sent and summed in bfloat16 or wider, within the bound.
A program may use at most 128 MiB of HBM per device.

```python
import jax
import jax.numpy as jnp
from jax import lax

MODEL_WIDTH = 2304
HIDDEN_UNITS = 4608
LATENTS = 65536
MINIBATCHES = 1
BATCH_TOKENS = 128
N_ROWS = 4


def level_of(rng, extent, shards, least, top_value):
    def one(dim, shards_of):
        heights = jax.random.uniform(jax.random.fold_in(jax.random.fold_in(rng, 6), dim), (shards_of,), jnp.float32, least / len(shards), top_value / len(shards))
        return jnp.repeat(jnp.exp(heights), extent[dim] // shards_of).reshape((-1,) + (1,) * (len(extent) - dim - 1))

    loudness = one(*shards[0])
    for cut in shards[1:]:
        loudness = loudness * one(*cut)
    return loudness


def noise(stream_key, extent, deviation, bound, cuts=(), dtype=jnp.bfloat16):
    result = jax.random.normal(stream_key, extent, jnp.float32) * deviation
    if len(cuts) > 0:
        result = level_of(stream_key, extent, cuts, -0.22, 0.18) * result
    return jnp.clip(result, min=-bound, max=bound).astype(dtype)


def setup_inputs(seed: int = 0, part: int = 0) -> dict:
    key_list = jax.random.split(jax.random.key(seed), 9)
    own_keys = jax.random.split(jax.random.fold_in(key_list[8], part), 9)
    return {
        "activations_in": noise(own_keys[0], (MINIBATCHES, BATCH_TOKENS, MODEL_WIDTH), 1.0, 6.0, ((2, 4),)),
        "gate_proj": noise(key_list[1], (MODEL_WIDTH, HIDDEN_UNITS), MODEL_WIDTH ** -0.5, 0.125, ((0, 4), (1, 4))),
        "up_proj": noise(key_list[2], (MODEL_WIDTH, HIDDEN_UNITS), MODEL_WIDTH ** -0.5, 0.125, ((0, 4), (1, 4))),
        "down_proj": noise(key_list[3], (HIDDEN_UNITS, MODEL_WIDTH), HIDDEN_UNITS ** -0.5, 0.09375, ((0, 4), (1, 4))),
        "enc_weight": noise(own_keys[4], (MODEL_WIDTH, LATENTS), 1.0, 6.0, ((0, 4), (1, 4))),
        "enc_bias": jnp.clip(jax.random.uniform(own_keys[5], (LATENTS,), jnp.float32, -0.5, 0.5) * level_of(own_keys[5], (LATENTS,), ((0, 4),), -0.4, 0.0), -0.5, 0.5),
        "dec_weight": noise(own_keys[6], (LATENTS, MODEL_WIDTH), 1.0, 6.0, ((0, 4), (1, 4))),
        "dec_bias": jnp.clip(jax.random.uniform(own_keys[7], (MODEL_WIDTH,), jnp.float32, -0.5, 0.5) * level_of(own_keys[7], (MODEL_WIDTH,), ((0, 4),), -0.4, 0.0), -0.5, 0.5),
    }


sparsity_cost = 0.1
sharpness = 8.0
weight_rate = 2.0
enc_bias_rate = 0.01
dec_bias_rate = 0.002


def smooth_relu(values):
    return jax.nn.softplus(sharpness * values) / sharpness


def reference(activations_in, gate_proj, up_proj, down_proj, enc_weight, enc_bias, dec_weight, dec_bias):
    flattened = activations_in.reshape(MINIBATCHES * BATCH_TOKENS, MODEL_WIDTH)
    gate_term = jnp.dot(flattened, gate_proj, preferred_element_type=jnp.float32)
    up_term = jnp.dot(flattened, up_proj, preferred_element_type=jnp.float32)
    hidden = (jax.nn.gelu(gate_term, approximate=True) * up_term).astype(jnp.bfloat16)
    features = jnp.dot(hidden, down_proj, preferred_element_type=jnp.float32).astype(jnp.bfloat16)
    features = features.reshape(MINIBATCHES, BATCH_TOKENS, MODEL_WIDTH)
    block_size = MODEL_WIDTH // N_ROWS
    enc_scale = MODEL_WIDTH ** -0.5
    dec_scale = LATENTS ** -0.5
    for batch_index in range(MINIBATCHES):
        inputs = features[batch_index]
        encoded = jnp.zeros((BATCH_TOKENS, LATENTS), jnp.float32)
        back_sum = jnp.zeros((BATCH_TOKENS, LATENTS), jnp.float32)
        for row_index in range(N_ROWS):
            lower = row_index * block_size
            term = jnp.dot(inputs[:, lower:lower + block_size], enc_weight[lower:lower + block_size],
                           preferred_element_type=jnp.float32).astype(jnp.bfloat16)
            encoded = encoded + lax.optimization_barrier(term).astype(jnp.float32)
        pre_latent = enc_scale * encoded + enc_bias
        latents = smooth_relu(pre_latent).astype(jnp.bfloat16)
        rebuilt = dec_scale * jnp.dot(latents, dec_weight, preferred_element_type=jnp.float32) + dec_bias
        residual_grad = (2.0 * (rebuilt - inputs.astype(jnp.float32))).astype(jnp.bfloat16)
        for row_index in range(N_ROWS):
            lower = row_index * block_size
            term = lax.dot_general(residual_grad[:, lower:lower + block_size], dec_weight[:, lower:lower + block_size],
                                   (((1,), (1,)), ((), ())), preferred_element_type=jnp.float32).astype(jnp.bfloat16)
            back_sum = back_sum + lax.optimization_barrier(term).astype(jnp.float32)
        latent_grad = (jax.nn.sigmoid(sharpness * pre_latent) * (dec_scale * back_sum + sparsity_cost)).astype(jnp.bfloat16)
        dec_grad = dec_scale * lax.dot_general(latents, residual_grad, (((0,), (0,)), ((), ())),
                                               preferred_element_type=jnp.float32)
        enc_grad = enc_scale * lax.dot_general(inputs, latent_grad, (((0,), (0,)), ((), ())),
                                               preferred_element_type=jnp.float32)
        enc_bias = enc_bias - enc_bias_rate * jnp.sum(latent_grad.astype(jnp.float32), axis=0)
        dec_bias = dec_bias - dec_bias_rate * jnp.sum(residual_grad.astype(jnp.float32), axis=0)
        enc_weight = (enc_weight.astype(jnp.float32) - weight_rate * enc_grad).astype(jnp.bfloat16)
        dec_weight = (dec_weight.astype(jnp.float32) - weight_rate * dec_grad).astype(jnp.bfloat16)
    return enc_weight, enc_bias, dec_weight, dec_bias
```

```python
import jax
import jax.numpy as jnp
from jax import lax
from jax.sharding import PartitionSpec as P

MODEL_WIDTH = 2304
LATENTS = 65536


sparsity_cost = 0.1
sharpness = 8.0
weight_rate = 2.0
enc_bias_rate = 0.01
dec_bias_rate = 0.002

BF16 = jnp.bfloat16
F32 = jnp.float32


def swap(x, axis, n, bit):
    return lax.ppermute(x, axis, [(i, i ^ bit) for i in range(n)])


def halves_scatter(x, axis, n, wire):
    me = lax.axis_index(axis)
    bit = 1
    while bit < n:
        size = x.shape[0] // 2
        mine = (me // bit) % 2
        keep = lax.dynamic_slice_in_dim(x, mine * size, size, 0)
        give = lax.dynamic_slice_in_dim(x, (1 - mine) * size, size, 0)
        got = swap(give.astype(wire), axis, n, bit)
        x = keep.astype(F32) + got.astype(F32)
        bit *= 2
    return x


def token_offset(axis, n, tokens):
    me = lax.axis_index(axis)
    offset, size, bit = 0, tokens, 1
    while bit < n:
        size //= 2
        offset = offset + ((me // bit) % 2) * size
        bit *= 2
    return offset, size


def halves_gather(x, axis, n):
    me = lax.axis_index(axis)
    bit = n // 2
    while bit >= 1:
        got = swap(x, axis, n, bit)
        first = ((me // bit) % 2) == 0
        x = jnp.concatenate([jnp.where(first, x, got), jnp.where(first, got, x)], axis=0)
        bit //= 2
    return x


def direct_scatter(x, axis, n, wire):
    me = lax.axis_index(axis)
    size = x.shape[0] // n
    total = lax.dynamic_slice_in_dim(x, me * size, size, 0)
    gots = []
    for shift in range(1, n):
        to = lax.rem(me + shift, n)
        give = lax.dynamic_slice_in_dim(x, to * size, size, 0).astype(wire)
        gots.append(lax.ppermute(give, axis, [(i, (i + shift) % n) for i in range(n)]))
    for got in gots:
        total = total + got.astype(F32)
    return total


def direct_gather(x, axis, n):
    me = lax.axis_index(axis)
    size = x.shape[0]
    out = jnp.zeros((size * n,) + x.shape[1:], x.dtype)
    parts = [(me, x)]
    for shift in range(1, n):
        got = lax.ppermute(x, axis, [(i, (i + shift) % n) for i in range(n)])
        parts.append((lax.rem(me - shift + n, n), got))
    for at, part in parts:
        out = lax.dynamic_update_slice_in_dim(out, part, at * size, 0)
    return out


def body(n_latent, n_rows, activations_in, gate_proj, up_proj, down_proj, enc_weight, enc_bias, dec_weight, dec_bias):
    tokens = activations_in.shape[1]
    width = enc_weight.shape[0]
    local = enc_weight.shape[1]
    here = activations_in.reshape(tokens, activations_in.shape[2])
    if n_latent == n_rows:
        pairs = [(a * n_rows + b, b * n_rows + a) for a in range(n_latent) for b in range(n_rows)]
        portion = lax.ppermute(here, ("latent", "rows"), pairs)
    else:
        everything = lax.all_gather(here, "latent", axis=1, tiled=True)
        portion = lax.dynamic_slice_in_dim(everything, lax.axis_index("rows") * width, width, 1)
    small = n_latent <= 8
    scatter_l = (lambda v: direct_scatter(v, "latent", n_latent, F32)) if small else (
        lambda v: lax.psum_scatter(v, "latent", scatter_dimension=0, tiled=True))
    gather_l = (lambda v: direct_gather(v, "latent", n_latent)) if small else (
        lambda v: lax.all_gather(v, "latent", axis=0, tiled=True))

    gate_part = jnp.dot(portion, gate_proj, preferred_element_type=F32)
    up_part = jnp.dot(portion, up_proj, preferred_element_type=F32)
    both = halves_scatter(jnp.concatenate([gate_part, up_part], axis=1), "rows", n_rows, F32)
    gate_term, up_term = both[:, :gate_proj.shape[1]], both[:, gate_proj.shape[1]:]
    hidden = (jax.nn.gelu(gate_term, approximate=True) * up_term).astype(BF16)
    hidden = halves_gather(hidden, "rows", n_rows)
    partial_value = jnp.dot(hidden, down_proj, preferred_element_type=F32)
    inputs_here = scatter_l(partial_value).astype(BF16)
    inputs = gather_l(inputs_here)

    enc_scale = MODEL_WIDTH ** (-0.5)
    dec_scale = LATENTS ** (-0.5)
    chunks = max(1, min(4, local // 512))
    step = local // chunks
    local_rebuilt = jnp.zeros((tokens, width), F32)
    latents, pres = [], []
    for c in range(chunks):
        part = jnp.dot(inputs, enc_weight[:, c * step:(c + 1) * step], preferred_element_type=F32).astype(BF16)
        encoded = halves_scatter(part, "rows", n_rows, BF16)
        pre = enc_scale * encoded + enc_bias[c * step:(c + 1) * step]
        pres.append(pre)
        mine = (jax.nn.softplus(sharpness * pre) / sharpness).astype(BF16)
        full = halves_gather(mine, "rows", n_rows)
        latents.append(full)
        local_rebuilt = local_rebuilt + jnp.dot(full, dec_weight[c * step:(c + 1) * step], preferred_element_type=F32)
    rebuilt_share = scatter_l(local_rebuilt)
    grad_share = (
        2.0 * (dec_scale * rebuilt_share + dec_bias - inputs_here.astype(F32))
    ).astype(BF16)
    residual_grad = gather_l(grad_share)
    grads = []
    for c in range(chunks):
        part = lax.dot_general(
            residual_grad, dec_weight[c * step:(c + 1) * step], (((1,), (1,)), ((), ())), preferred_element_type=F32
        ).astype(BF16)
        back = halves_scatter(part, "rows", n_rows, BF16)
        mine = (jax.nn.sigmoid(sharpness * pres[c]) * (dec_scale * back + sparsity_cost)).astype(BF16)
        grads.append(halves_gather(mine, "rows", n_rows))
    latents = jnp.concatenate(latents, axis=1)
    latent_grad = jnp.concatenate(grads, axis=1)
    dec_grad = dec_scale * lax.dot_general(
        latents, residual_grad, (((0,), (0,)), ((), ())), preferred_element_type=F32
    )
    enc_grad = enc_scale * lax.dot_general(
        inputs, latent_grad, (((0,), (0,)), ((), ())), preferred_element_type=F32
    )
    enc_bias = enc_bias - enc_bias_rate * jnp.sum(latent_grad, axis=0, dtype=F32)
    dec_bias = dec_bias - dec_bias_rate * jnp.sum(residual_grad, axis=0, dtype=F32)
    enc_weight = (enc_weight.astype(F32) - weight_rate * enc_grad).astype(BF16)
    dec_weight = (dec_weight.astype(F32) - weight_rate * dec_grad).astype(BF16)
    return (enc_weight, enc_bias, dec_weight, dec_bias)


def solution(mesh):
    def step(*args):
        return body(mesh.shape["latent"], mesh.shape["rows"], *args)

    return jax.shard_map(
        step,
        mesh=mesh,
        in_specs=(
            P("groups", None, "latent"),
            P("rows", "latent"),
            P("rows", "latent"),
            P("latent", "rows"),
            P(("groups", "rows"), "latent"),
            P(("groups", "latent")),
            P(("groups", "latent"), "rows"),
            P(("groups", "rows")),
        ),
        out_specs=(
            P(("groups", "rows"), "latent"),
            P(("groups", "latent")),
            P(("groups", "latent"), "rows"),
            P(("groups", "rows")),
        ),
        check_vma=False,
    )
```

```python
import functools

import jax
import jax.numpy as jnp
from jax import lax
from jax.experimental import pallas as pl
from jax.experimental.pallas import tpu as pltpu
from jax.sharding import PartitionSpec as P

MODEL_WIDTH = 2304
LATENTS = 65536


sparsity_cost = 0.1
sharpness = 8.0
weight_rate = 2.0
enc_bias_rate = 0.01
dec_bias_rate = 0.002

BF16 = jnp.bfloat16
F32 = jnp.float32


def swap(x, axis, n, bit):
    return lax.ppermute(x, axis, [(i, i ^ bit) for i in range(n)])


def halves_scatter(x, axis, n, wire):
    me = lax.axis_index(axis)
    bit = 1
    while bit < n:
        size = x.shape[0] // 2
        mine = (me // bit) % 2
        keep = lax.dynamic_slice_in_dim(x, mine * size, size, 0)
        give = lax.dynamic_slice_in_dim(x, (1 - mine) * size, size, 0)
        got = swap(give.astype(wire), axis, n, bit)
        x = keep.astype(F32) + got.astype(F32)
        bit *= 2
    return x


def halves_gather(x, axis, n):
    me = lax.axis_index(axis)
    bit = n // 2
    while bit >= 1:
        got = swap(x, axis, n, bit)
        first = ((me // bit) % 2) == 0
        x = jnp.concatenate([jnp.where(first, x, got), jnp.where(first, got, x)], axis=0)
        bit //= 2
    return x


def direct_scatter(x, axis, n, wire):
    me = lax.axis_index(axis)
    size = x.shape[0] // n
    total = lax.dynamic_slice_in_dim(x, me * size, size, 0)
    gots = []
    for shift in range(1, n):
        to = lax.rem(me + shift, n)
        give = lax.dynamic_slice_in_dim(x, to * size, size, 0).astype(wire)
        gots.append(lax.ppermute(give, axis, [(i, (i + shift) % n) for i in range(n)]))
    for got in gots:
        total = total + got.astype(F32)
    return total


def direct_gather(x, axis, n):
    me = lax.axis_index(axis)
    size = x.shape[0]
    out = jnp.zeros((size * n,) + x.shape[1:], x.dtype)
    parts = [(me, x)]
    for shift in range(1, n):
        got = lax.ppermute(x, axis, [(i, (i + shift) % n) for i in range(n)])
        parts.append((lax.rem(me - shift + n, n), got))
    for at, part in parts:
        out = lax.dynamic_update_slice_in_dim(out, part, at * size, 0)
    return out


def update_kernel(rate, has_buf, left_ref, right_ref, w_ref, *rest):
    out_ref, sums_ref = rest[1:] if has_buf else rest
    right = right_ref[...]
    grad = jnp.dot(left_ref[...], right, preferred_element_type=F32)
    out_ref[...] = (w_ref[...].astype(F32) - rate * grad).astype(out_ref.dtype)
    ones = jnp.ones((8, right.shape[0]), right.dtype)
    sums_ref[...] = jnp.dot(ones, right, preferred_element_type=F32)


def update(rate, left, right, weight, first, buf):
    depth, tokens = left.shape
    columns = right.shape[1]
    tile = min(2048, columns)
    base = first // tile
    block = pl.BlockSpec((depth, tile), lambda i: (0, base + i))
    in_specs = [
        pl.BlockSpec((depth, tokens), lambda i: (0, 0)),
        pl.BlockSpec((tokens, tile), lambda i: (0, i)),
        block,
    ]
    args = [left, right, weight]
    if buf is not None:
        in_specs.append(pl.BlockSpec(memory_space=pl.ANY))
        args.append(buf)
    return pl.pallas_call(
        functools.partial(update_kernel, rate, buf is not None),
        grid=(columns // tile,),
        out_shape=(
            jax.ShapeDtypeStruct(weight.shape, weight.dtype),
            jax.ShapeDtypeStruct((8, columns), F32),
        ),
        in_specs=in_specs,
        out_specs=(block, pl.BlockSpec((8, tile), lambda i: (0, i))),
        input_output_aliases={} if buf is None else {3: 0},
        compiler_params=pltpu.CompilerParams(vmem_limit_bytes=24 * 1024 * 1024),
        cost_estimate=pl.CostEstimate(
            flops=2 * depth * tokens * columns, bytes_accessed=4 * depth * columns, transcendentals=0
        ),
    )(*args)


def body(n_latent, n_rows, activations_in, gate_proj, up_proj, down_proj, enc_weight, enc_bias, dec_weight, dec_bias):
    tokens = activations_in.shape[1]
    width, local = enc_weight.shape
    here = activations_in.reshape(tokens, activations_in.shape[2])
    if n_latent == n_rows:
        pairs = [(a * n_rows + b, b * n_rows + a) for a in range(n_latent) for b in range(n_rows)]
        portion = lax.ppermute(here, ("latent", "rows"), pairs)
    else:
        everything = lax.all_gather(here, "latent", axis=1, tiled=True)
        portion = lax.dynamic_slice_in_dim(everything, lax.axis_index("rows") * width, width, 1)
    if n_latent <= 8:
        scatter_l = lambda v, wire: direct_scatter(v, "latent", n_latent, wire)
        gather_l = lambda v: direct_gather(v, "latent", n_latent)
    else:
        scatter_l = lambda v, wire: lax.psum_scatter(v, "latent", scatter_dimension=0, tiled=True)
        gather_l = lambda v: lax.all_gather(v, "latent", axis=0, tiled=True)

    gate_part = jnp.dot(portion, gate_proj, preferred_element_type=F32)
    up_part = jnp.dot(portion, up_proj, preferred_element_type=F32)
    both = jnp.concatenate([gate_part, up_part], axis=1).astype(BF16)
    both = halves_scatter(both, "rows", n_rows, BF16)
    gate_term, up_term = both[:, :gate_proj.shape[1]], both[:, gate_proj.shape[1]:]
    hidden = (jax.nn.gelu(gate_term, approximate=True) * up_term).astype(BF16)
    hidden = halves_gather(hidden, "rows", n_rows)
    partial_value = lax.dot_general(down_proj, hidden, (((0,), (1,)), ((), ())), preferred_element_type=F32)
    inputs_here = scatter_l(partial_value, BF16).astype(BF16)
    inputs = gather_l(inputs_here)
    share = inputs_here.shape[0]
    bias_here = lax.dynamic_slice_in_dim(dec_bias, lax.axis_index("latent") * share, share, 0)

    enc_scale = MODEL_WIDTH ** (-0.5)
    dec_scale = LATENTS ** (-0.5)
    dec_turned = dec_weight.T
    chunks = max(1, min(4, local // 512))
    step = local // chunks
    spans = [slice(c * step, (c + 1) * step) for c in range(chunks)]
    over_width = (((0,), (0,)), ((), ()))
    local_rebuilt = jnp.zeros((width, tokens), F32)
    latents, pres = [], []
    for span in spans:
        part = lax.dot_general(inputs, enc_weight[:, span], over_width, preferred_element_type=F32).astype(BF16)
        encoded = halves_scatter(part, "rows", n_rows, BF16)
        pre = enc_scale * encoded + enc_bias[span]
        pres.append(pre)
        mine = (jax.nn.softplus(sharpness * pre) / sharpness).astype(BF16)
        full = halves_gather(mine, "rows", n_rows)
        latents.append(full)
        local_rebuilt = local_rebuilt + lax.dot_general(
            dec_turned[:, span], full, (((1,), (1,)), ((), ())), preferred_element_type=F32
        )
    rebuilt_share = scatter_l(local_rebuilt, F32)
    grad_share = (
        2.0 * (dec_scale * rebuilt_share + bias_here[:, None] - inputs_here.astype(F32))
    ).astype(BF16)
    residual_grad = gather_l(grad_share)
    grads = []
    for c, span in enumerate(spans):
        part = lax.dot_general(residual_grad, dec_turned[:, span], over_width, preferred_element_type=F32).astype(BF16)
        back = halves_scatter(part, "rows", n_rows, BF16)
        mine = (jax.nn.sigmoid(sharpness * pres[c]) * (dec_scale * back + sparsity_cost)).astype(BF16)
        grads.append(halves_gather(mine, "rows", n_rows))
    dec_new = enc_new = None
    for c, span in enumerate(spans):
        dec_new, _ = update(weight_rate * dec_scale, residual_grad, latents[c], dec_turned, c * step, dec_new)
    sums = []
    for c, span in enumerate(spans):
        enc_new, total = update(weight_rate * enc_scale, inputs, grads[c], enc_weight, c * step, enc_new)
        sums.append(total[0])
    enc_bias = enc_bias - enc_bias_rate * jnp.concatenate(sums)
    dec_bias = dec_bias - dec_bias_rate * jnp.sum(residual_grad, axis=1, dtype=F32)
    return (enc_new, enc_bias, dec_new.T, dec_bias)


def solution(mesh):
    def step(*args):
        return body(mesh.shape["latent"], mesh.shape["rows"], *args)


    return jax.shard_map(
        step,
        mesh=mesh,
        in_specs=(
            P("groups", None, "latent"),
            P("rows", "latent"),
            P("rows", "latent"),
            P("latent", "rows"),
            P(("groups", "rows"), "latent"),
            P(("groups", "latent")),
            P(("groups", "latent"), "rows"),
            P(("groups", "rows")),
        ),
        out_specs=(
            P(("groups", "rows"), "latent"),
            P(("groups", "latent")),
            P(("groups", "latent"), "rows"),
            P(("groups", "rows")),
        ),
        check_vma=False,
    )
```

```python
import functools

import jax
import jax.numpy as jnp
from jax import lax
from jax.experimental import pallas as pl
from jax.experimental.pallas import tpu as pltpu
from jax.sharding import PartitionSpec as P

MODEL_WIDTH = 2304
LATENTS = 65536


sparsity_cost = 0.1
sharpness = 8.0
weight_rate = 2.0
enc_bias_rate = 0.01
dec_bias_rate = 0.002

BF16 = jnp.bfloat16
F32 = jnp.float32


def swap(x, axis, n, bit):
    return lax.ppermute(x, axis, [(i, i ^ bit) for i in range(n)])


def halves_scatter(x, axis, n, wire):
    me = lax.axis_index(axis)
    bit = 1
    while bit < n:
        size = x.shape[0] // 2
        mine = (me // bit) % 2
        keep = lax.dynamic_slice_in_dim(x, mine * size, size, 0)
        give = lax.dynamic_slice_in_dim(x, (1 - mine) * size, size, 0)
        got = swap(give.astype(wire), axis, n, bit)
        x = keep.astype(F32) + got.astype(F32)
        bit *= 2
    return x


def halves_gather(x, axis, n):
    me = lax.axis_index(axis)
    bit = n // 2
    while bit >= 1:
        got = swap(x, axis, n, bit)
        first = ((me // bit) % 2) == 0
        x = jnp.concatenate([jnp.where(first, x, got), jnp.where(first, got, x)], axis=0)
        bit //= 2
    return x


def direct_scatter(x, axis, n, wire):
    me = lax.axis_index(axis)
    size = x.shape[0] // n
    total = lax.dynamic_slice_in_dim(x, me * size, size, 0)
    gots = []
    for shift in range(1, n):
        to = lax.rem(me + shift, n)
        give = lax.dynamic_slice_in_dim(x, to * size, size, 0).astype(wire)
        gots.append(lax.ppermute(give, axis, [(i, (i + shift) % n) for i in range(n)]))
    for got in gots:
        total = total + got.astype(F32)
    return total


def direct_gather(x, axis, n):
    me = lax.axis_index(axis)
    size = x.shape[0]
    out = jnp.zeros((size * n,) + x.shape[1:], x.dtype)
    parts = [(me, x)]
    for shift in range(1, n):
        got = lax.ppermute(x, axis, [(i, (i + shift) % n) for i in range(n)])
        parts.append((lax.rem(me - shift + n, n), got))
    for at, part in parts:
        out = lax.dynamic_update_slice_in_dim(out, part, at * size, 0)
    return out


def update_kernel(rate, has_buf, left_ref, right_ref, w_ref, *rest):
    out_ref, sums_ref = rest[1:] if has_buf else rest
    right = right_ref[...]
    grad = jnp.dot(left_ref[...], right, preferred_element_type=F32)
    out_ref[...] = (w_ref[...].astype(F32) - rate * grad).astype(out_ref.dtype)
    ones = jnp.ones((8, right.shape[0]), right.dtype)
    sums_ref[...] = jnp.dot(ones, right, preferred_element_type=F32)


def update(rate, left, right, weight, first, buf, grant):
    depth, tokens = left.shape
    columns = right.shape[1]
    tile = min(2048, columns)
    base = first // tile
    block = pl.BlockSpec((depth, tile), lambda i: (0, base + i))
    in_specs = [
        pl.BlockSpec((depth, tokens), lambda i: (0, 0)),
        pl.BlockSpec((tokens, tile), lambda i: (0, i)),
        block,
    ]
    args = [left, right, weight]
    if buf is not None:
        in_specs.append(pl.BlockSpec(memory_space=pl.ANY))
        args.append(buf)
    return pl.pallas_call(
        functools.partial(update_kernel, rate, buf is not None),
        grid=(columns // tile,),
        out_shape=(
            jax.ShapeDtypeStruct(weight.shape, weight.dtype),
            jax.ShapeDtypeStruct((8, columns), F32),
        ),
        in_specs=in_specs,
        out_specs=(block, pl.BlockSpec((8, tile), lambda i: (0, i))),
        input_output_aliases={} if buf is None else {3: 0},
        compiler_params=pltpu.CompilerParams(vmem_limit_bytes=grant),
        cost_estimate=pl.CostEstimate(
            flops=2 * depth * tokens * columns, bytes_accessed=4 * depth * columns, transcendentals=0
        ),
    )(*args)


def body(n_latent, n_rows, activations_in, gate_proj, up_proj, down_proj, enc_weight, enc_bias, dec_weight, dec_bias):
    tokens = activations_in.shape[1]
    width, local = enc_weight.shape
    here = activations_in.reshape(tokens, activations_in.shape[2])
    if n_latent == n_rows:
        pairs = [(a * n_rows + b, b * n_rows + a) for a in range(n_latent) for b in range(n_rows)]
        portion = lax.ppermute(here, ("latent", "rows"), pairs)
    else:
        everything = lax.all_gather(here, "latent", axis=1, tiled=True)
        portion = lax.dynamic_slice_in_dim(everything, lax.axis_index("rows") * width, width, 1)
    if n_latent <= 8:
        scatter_l = lambda v, wire: direct_scatter(v, "latent", n_latent, wire)
        gather_l = lambda v: direct_gather(v, "latent", n_latent)
    else:
        scatter_l = lambda v, wire: lax.psum_scatter(v, "latent", scatter_dimension=0, tiled=True)
        gather_l = lambda v: lax.all_gather(v, "latent", axis=0, tiled=True)

    gate_part = jnp.dot(portion, gate_proj, preferred_element_type=F32)
    up_part = jnp.dot(portion, up_proj, preferred_element_type=F32)
    both = jnp.concatenate([gate_part, up_part], axis=1).astype(BF16)
    both = halves_scatter(both, "rows", n_rows, BF16)
    gate_term, up_term = both[:, :gate_proj.shape[1]], both[:, gate_proj.shape[1]:]
    hidden = (jax.nn.gelu(gate_term, approximate=True) * up_term).astype(BF16)
    hidden = halves_gather(hidden, "rows", n_rows)
    partial_value = lax.dot_general(down_proj, hidden, (((0,), (1,)), ((), ())), preferred_element_type=F32)
    inputs_here = scatter_l(partial_value, BF16).astype(BF16)
    inputs = gather_l(inputs_here)
    share = inputs_here.shape[0]
    bias_here = lax.dynamic_slice_in_dim(dec_bias, lax.axis_index("latent") * share, share, 0)

    enc_scale = MODEL_WIDTH ** (-0.5)
    dec_scale = LATENTS ** (-0.5)
    dec_turned = dec_weight.T
    chunks = max(1, min(4, local // 512))
    step = local // chunks
    spans = [slice(c * step, (c + 1) * step) for c in range(chunks)]
    over_width = (((0,), (0,)), ((), ()))
    local_rebuilt = jnp.zeros((width, tokens), F32)
    latents, pres = [], []
    for span in spans:
        part = lax.dot_general(inputs, enc_weight[:, span], over_width, preferred_element_type=F32).astype(BF16)
        encoded = halves_scatter(part, "rows", n_rows, BF16)
        pre = enc_scale * encoded + enc_bias[span]
        pres.append(pre)
        mine = (jax.nn.softplus(sharpness * pre) / sharpness).astype(BF16)
        full = halves_gather(mine, "rows", n_rows)
        latents.append(full)
        local_rebuilt = local_rebuilt + lax.dot_general(
            dec_turned[:, span], full, (((1,), (1,)), ((), ())), preferred_element_type=F32
        )
    rebuilt_share = scatter_l(local_rebuilt, F32)
    grad_share = (
        2.0 * (dec_scale * rebuilt_share + bias_here[:, None] - inputs_here.astype(F32))
    ).astype(BF16)
    residual_grad = gather_l(grad_share)
    grads = []
    for c, span in enumerate(spans):
        part = lax.dot_general(residual_grad, dec_turned[:, span], over_width, preferred_element_type=F32).astype(BF16)
        back = halves_scatter(part, "rows", n_rows, BF16)
        mine = (jax.nn.sigmoid(sharpness * pres[c]) * (dec_scale * back + sparsity_cost)).astype(BF16)
        grads.append(halves_gather(mine, "rows", n_rows))
    dec_new = enc_new = None
    for c, span in enumerate(spans):
        dec_new, _ = update(weight_rate * dec_scale, residual_grad, latents[c], dec_turned, c * step, dec_new, 24 << 20)
    sums = []
    for c, span in enumerate(spans):
        enc_new, total = update(weight_rate * enc_scale, inputs, grads[c], enc_weight, c * step, enc_new, 52 << 20)
        sums.append(total[0])
    enc_bias = enc_bias - enc_bias_rate * jnp.concatenate(sums)
    dec_bias = dec_bias - dec_bias_rate * jnp.sum(residual_grad, axis=1, dtype=F32)
    return (enc_new, enc_bias, dec_new.T, dec_bias)


def solution(mesh):
    def step(*args):
        return body(mesh.shape["latent"], mesh.shape["rows"], *args)


    return jax.shard_map(
        step,
        mesh=mesh,
        in_specs=(
            P("groups", None, "latent"),
            P("rows", "latent"),
            P("rows", "latent"),
            P("latent", "rows"),
            P(("groups", "rows"), "latent"),
            P(("groups", "latent")),
            P(("groups", "latent"), "rows"),
            P(("groups", "rows")),
        ),
        out_specs=(
            P(("groups", "rows"), "latent"),
            P(("groups", "latent")),
            P(("groups", "latent"), "rows"),
            P(("groups", "rows")),
        ),
        check_vma=False,
    )
```

```python
import functools

import jax
import jax.numpy as jnp
from jax import lax
from jax.experimental import pallas as pl
from jax.experimental.pallas import tpu as pltpu
from jax.sharding import PartitionSpec as P

MODEL_WIDTH = 2304
LATENTS = 65536


sparsity_cost = 0.1
sharpness = 8.0
weight_rate = 2.0
enc_bias_rate = 0.01
dec_bias_rate = 0.002

BF16 = jnp.bfloat16
F32 = jnp.float32


def swap(x, axis, n, bit):
    return lax.ppermute(x, axis, [(i, i ^ bit) for i in range(n)])


def halves_scatter(x, axis, n, wire):
    me = lax.axis_index(axis)
    bit = 1
    while bit < n:
        size = x.shape[0] // 2
        mine = (me // bit) % 2
        keep = lax.dynamic_slice_in_dim(x, mine * size, size, 0)
        give = lax.dynamic_slice_in_dim(x, (1 - mine) * size, size, 0)
        got = swap(give.astype(wire), axis, n, bit)
        x = keep.astype(F32) + got.astype(F32)
        bit *= 2
    return x


def halves_gather(x, axis, n, ordered=True):
    me = lax.axis_index(axis)
    bit = n // 2
    while bit >= 1:
        got = swap(x, axis, n, bit)
        if not ordered:
            x = jnp.concatenate([x, got], axis=0)
            bit //= 2
            continue
        first = ((me // bit) % 2) == 0
        x = jnp.concatenate([jnp.where(first, x, got), jnp.where(first, got, x)], axis=0)
        bit //= 2
    return x


def own_first(x, axis, n):
    me = lax.axis_index(axis)
    bit, size = 1, x.shape[1]
    while bit < n:
        half = size // 2
        split = x.reshape(x.shape[0], -1, 2, half)
        x = jnp.where(((me // bit) % 2) == 0, split, split[:, :, ::-1]).reshape(x.shape)
        bit, size = bit * 2, half
    return x


def direct_scatter(x, axis, n, wire):
    me = lax.axis_index(axis)
    size = x.shape[0] // n
    total = lax.dynamic_slice_in_dim(x, me * size, size, 0)
    gots = []
    for shift in range(1, n):
        to = lax.rem(me + shift, n)
        give = lax.dynamic_slice_in_dim(x, to * size, size, 0).astype(wire)
        gots.append(lax.ppermute(give, axis, [(i, (i + shift) % n) for i in range(n)]))
    for got in gots:
        total = total + got.astype(F32)
    return total


def direct_gather(x, axis, n):
    me = lax.axis_index(axis)
    size = x.shape[0]
    out = jnp.zeros((size * n,) + x.shape[1:], x.dtype)
    parts = [(me, x)]
    for shift in range(1, n):
        got = lax.ppermute(x, axis, [(i, (i + shift) % n) for i in range(n)])
        parts.append((lax.rem(me - shift + n, n), got))
    for at, part in parts:
        out = lax.dynamic_update_slice_in_dim(out, part, at * size, 0)
    return out


def update_kernel(rate, has_buf, left_ref, right_ref, w_ref, *rest):
    out_ref, sums_ref = rest[1:] if has_buf else rest
    right = right_ref[...]
    grad = jnp.dot(left_ref[...], right, preferred_element_type=F32)
    out_ref[...] = (w_ref[...].astype(F32) - rate * grad).astype(out_ref.dtype)
    ones = jnp.ones((8, right.shape[0]), right.dtype)
    sums_ref[...] = jnp.dot(ones, right, preferred_element_type=F32)


def update(rate, left, right, weight, first, buf, grant):
    depth, tokens = left.shape
    columns = right.shape[1]
    tile = min(512, columns)
    base = first // tile
    block = pl.BlockSpec((depth, tile), lambda i: (0, base + i))
    in_specs = [
        pl.BlockSpec((depth, tokens), lambda i: (0, 0)),
        pl.BlockSpec((tokens, tile), lambda i: (0, i)),
        block,
    ]
    args = [left, right, weight]
    if buf is not None:
        in_specs.append(pl.BlockSpec(memory_space=pl.ANY))
        args.append(buf)
    return pl.pallas_call(
        functools.partial(update_kernel, rate, buf is not None),
        grid=(columns // tile,),
        out_shape=(
            jax.ShapeDtypeStruct(weight.shape, weight.dtype),
            jax.ShapeDtypeStruct((8, columns), F32),
        ),
        in_specs=in_specs,
        out_specs=(block, pl.BlockSpec((8, tile), lambda i: (0, i))),
        input_output_aliases={} if buf is None else {3: 0},
        compiler_params=pltpu.CompilerParams(vmem_limit_bytes=grant),
        cost_estimate=pl.CostEstimate(
            flops=2 * depth * tokens * columns, bytes_accessed=4 * depth * columns, transcendentals=0
        ),
    )(*args)


def body(n_latent, n_rows, activations_in, gate_proj, up_proj, down_proj, enc_weight, enc_bias, dec_weight, dec_bias):
    tokens = activations_in.shape[1]
    width, local = enc_weight.shape
    here = activations_in.reshape(tokens, activations_in.shape[2])
    if n_latent == n_rows:
        pairs = [(a * n_rows + b, b * n_rows + a) for a in range(n_latent) for b in range(n_rows)]
        portion = lax.ppermute(here, ("latent", "rows"), pairs)
    else:
        everything = lax.all_gather(here, "latent", axis=1, tiled=True)
        portion = lax.dynamic_slice_in_dim(everything, lax.axis_index("rows") * width, width, 1)
    if n_latent <= 8:
        scatter_l = lambda v, wire: direct_scatter(v, "latent", n_latent, wire)
        gather_l = lambda v: direct_gather(v, "latent", n_latent)
    else:
        scatter_l = lambda v, wire: lax.psum_scatter(v, "latent", scatter_dimension=0, tiled=True)
        gather_l = lambda v: lax.all_gather(v, "latent", axis=0, tiled=True)

    gate_part = jnp.dot(portion, gate_proj, preferred_element_type=F32)
    up_part = jnp.dot(portion, up_proj, preferred_element_type=F32)
    both = jnp.concatenate([gate_part, up_part], axis=1).astype(BF16)
    both = halves_scatter(both, "rows", n_rows, BF16)
    gate_term, up_term = both[:, :gate_proj.shape[1]], both[:, gate_proj.shape[1]:]
    hidden = (jax.nn.gelu(gate_term, approximate=True) * up_term).astype(BF16)
    hidden = halves_gather(hidden, "rows", n_rows)
    partial_value = lax.dot_general(down_proj, hidden, (((0,), (1,)), ((), ())), preferred_element_type=F32)
    inputs_here = scatter_l(partial_value, BF16).astype(BF16)
    inputs = gather_l(inputs_here)
    share = inputs_here.shape[0]
    bias_here = lax.dynamic_slice_in_dim(dec_bias, lax.axis_index("latent") * share, share, 0)

    enc_scale = MODEL_WIDTH ** (-0.5)
    dec_scale = LATENTS ** (-0.5)
    dec_turned = dec_weight.T
    chunks = max(1, min(4, local // 512))
    step = local // chunks
    spans = [slice(c * step, (c + 1) * step) for c in range(chunks)]
    over_width = (((0,), (0,)), ((), ()))
    local_rebuilt = jnp.zeros((width, tokens), F32)
    latents, pres = [], []
    for span in spans:
        part = lax.dot_general(inputs, enc_weight[:, span], over_width, preferred_element_type=F32).astype(BF16)
        encoded = halves_scatter(part, "rows", n_rows, BF16)
        pre = enc_scale * encoded + enc_bias[span]
        pres.append(pre)
        mine = (jax.nn.softplus(sharpness * pre) / sharpness).astype(BF16)
        full = halves_gather(mine, "rows", n_rows)
        latents.append(full)
        local_rebuilt = local_rebuilt + lax.dot_general(
            dec_turned[:, span], full, (((1,), (1,)), ((), ())), preferred_element_type=F32
        )
    rebuilt_share = scatter_l(local_rebuilt, F32)
    grad_share = (
        2.0 * (dec_scale * rebuilt_share + bias_here[:, None] - inputs_here.astype(F32))
    ).astype(BF16)
    residual_grad = gather_l(grad_share)
    grads = []
    for c, span in enumerate(spans):
        part = lax.dot_general(residual_grad, dec_turned[:, span], over_width, preferred_element_type=F32).astype(BF16)
        back = halves_scatter(part, "rows", n_rows, BF16)
        mine = (jax.nn.sigmoid(sharpness * pres[c]) * (dec_scale * back + sparsity_cost)).astype(BF16)
        grads.append(halves_gather(mine, "rows", n_rows, ordered=False))
    dec_new = enc_new = None
    for c, span in enumerate(spans):
        dec_new, _ = update(weight_rate * dec_scale, residual_grad, latents[c], dec_turned, c * step, dec_new, 24 << 20)
    sums = []
    turned_inputs = own_first(inputs, "rows", n_rows)
    for c, span in enumerate(spans):
        enc_new, total = update(weight_rate * enc_scale, turned_inputs, grads[c], enc_weight, c * step, enc_new, 52 << 20)
        sums.append(total[0])
    enc_bias = enc_bias - enc_bias_rate * jnp.concatenate(sums)
    dec_bias = dec_bias - dec_bias_rate * jnp.sum(residual_grad, axis=1, dtype=F32)
    return (enc_new, enc_bias, dec_new.T, dec_bias)


def solution(mesh):
    def step(*args):
        return body(mesh.shape["latent"], mesh.shape["rows"], *args)


    return jax.shard_map(
        step,
        mesh=mesh,
        in_specs=(
            P("groups", None, "latent"),
            P("rows", "latent"),
            P("rows", "latent"),
            P("latent", "rows"),
            P(("groups", "rows"), "latent"),
            P(("groups", "latent")),
            P(("groups", "latent"), "rows"),
            P(("groups", "rows")),
        ),
        out_specs=(
            P(("groups", "rows"), "latent"),
            P(("groups", "latent")),
            P(("groups", "latent"), "rows"),
            P(("groups", "rows")),
        ),
        check_vma=False,
    )
```
